256 devices in a mesh: pair: 32 (over y, z), seg: 8 (over x, core).
Axes of the slice: x: 4, y: 4, z: 8, core: 2. Of those that a mesh axis runs over, the one named last changes fastest.
Arguments:
- spectra: bfloat16 [768, 4096, 128], P('seg', 'pair'), may hold values from -240 to 240
- pair_lists: int32 [32, 2, 2], P('pair'), may hold values from -1 to 31, as said below
- distance_mask: int32 [512], replicated, may hold values 0 or 1
Outputs:
- correlations: bfloat16 [32, 2, 128, 128, 1025], P('pair', None, 'seg')
The draws below stay inside these ranges and needn't reach their ends.
Inputs may be any that keep to these rules, and one draw needn't show every extreme that they name: `pair_lists`: for device q (the index along the first dimension), each slot holds (r, c) with q <= r <= c <= min(q + 3, 31), or (-1, -1) for an empty slot; slot 0 of every device is never empty.
All inputs are finite; a program needn't handle non-finite values.
Results may differ from the reference program's by a relative error of at most 0.014.
Values may be sent and summed in bfloat16 or wider, within the bound.
A program may use at most 256 MiB of HBM per device.

```python
import math
import jax
import jax.numpy as jnp
from jax import lax

CB = 128
F = 64
LAGS = 1025
SAMPLES = 6000
FIRST_BIN = 30
SMOOTH = 4
BAND_BLOCKS = 4
SLOTS = 2
SEG_DEV = 96
SEGS = 768
CHANNELS = 4096
N_PAIR = 32
N_SEG = 8


def draw_spectra(key, part):
    subkeys = jax.random.split(key, 3)
    channel_scale = jnp.exp(jax.random.uniform(subkeys[0], (1, CHANNELS, 1), jnp.float32) * math.log(10.0))
    base_value = jnp.clip(jax.random.normal(subkeys[2], (SEGS, CHANNELS, 2 * F), jnp.float32), -6.0, 6.0)
    cell_scale = jnp.exp(jax.random.uniform(subkeys[1], (SEGS, CHANNELS, F), jnp.float32) * math.log(4.0))
    cell_both = jnp.concatenate([cell_scale, cell_scale], -1)
    return (base_value * cell_both * channel_scale).astype(jnp.bfloat16)


def draw_pair_lists(key, part):
    subkeys = jax.random.split(key, 3)
    device = jnp.arange(N_PAIR, dtype=jnp.int32)[:, None]
    col_offset = jax.random.randint(subkeys[0], (N_PAIR, SLOTS), 0, BAND_BLOCKS, jnp.int32)
    col_offset = jnp.minimum(col_offset, N_PAIR - 1 - device)
    row_raw = jax.random.randint(subkeys[1], (N_PAIR, SLOTS), 0, BAND_BLOCKS, jnp.int32)
    row_offset = row_raw % (col_offset + 1)
    active = jax.random.randint(subkeys[2], (N_PAIR, SLOTS), 0, 4, jnp.int32) > 0
    active = jnp.logical_or(active, (jnp.arange(SLOTS, dtype=jnp.int32) == 0)[None, :])
    row_block = jnp.where(active, device + row_offset, -1)
    col_block = jnp.where(active, device + col_offset, -1)
    return jnp.stack([row_block, col_block], -1).astype(jnp.int32)


def touch_ends(values, own_key, least, high):
    extent = values.shape
    spot = [jax.random.randint(jax.random.fold_in(own_key, axis), (), 0, extent[axis]) for axis in range(len(extent))]
    values = values.at[tuple(spot)].set(least)
    longest = extent.index(max(extent))
    spot[longest] = (spot[longest] + 1) % extent[longest]
    return values.at[tuple(spot)].set(high)


def setup_inputs(seed: int = 0) -> dict:
    key_of = jax.random.split(jax.random.key(seed), 4)
    return {
        "spectra": draw_spectra(jax.random.fold_in(key_of[3], 71), 0),
        "pair_lists": draw_pair_lists(jax.random.fold_in(key_of[3], 71), 0),
        "distance_mask": touch_ends((jax.random.randint(key_of[2], (BAND_BLOCKS * CB,), 0, 4) < 3).astype(jnp.int32), jax.random.fold_in(key_of[2], 1), 0, 1),
    }


def whiten(spectra):
    bin_count = spectra.shape[-1] // 2
    as_float = spectra.astype(jnp.float32)
    real_part = as_float[..., :bin_count]
    imag_part = as_float[..., bin_count:]
    amplitude = jnp.sqrt(real_part * real_part + imag_part * imag_part + 1e-06)
    positions = jnp.arange(bin_count, dtype=jnp.int32)
    inside = (jnp.abs(positions[:, None] - positions[None, :]) <= SMOOTH).astype(jnp.float32)
    smoothing = inside / lax.optimization_barrier(jnp.sum(inside, axis=0, keepdims=True))
    smoothed = jnp.matmul(amplitude, smoothing, precision=lax.Precision.HIGHEST)
    return jnp.concatenate([real_part / smoothed, imag_part / smoothed], -1).astype(jnp.bfloat16)

def lag_weights(bin_count, lag_count):
    frequency = jnp.arange(bin_count, dtype=jnp.int32) + FIRST_BIN
    lag_index = jnp.arange(lag_count, dtype=jnp.int32) - lag_count // 2
    phase_index = frequency[:, None] * lag_index[None, :] % SAMPLES
    theta = phase_index.astype(jnp.float32) * (2.0 * math.pi / SAMPLES)
    return jnp.concatenate([jnp.cos(theta), -jnp.sin(theta)], 0).astype(jnp.bfloat16)

def distance_factor(distance_mask, row_first, row_total, block_gap, col_total):
    row_ids = row_first + jnp.arange(row_total, dtype=jnp.int32)
    col_ids = jnp.arange(col_total, dtype=jnp.int32)
    distance = jnp.abs(col_total * block_gap + col_ids[None, :] - row_ids[:, None]).reshape(-1)
    matches = (distance[:, None] == jnp.arange(distance_mask.shape[0], dtype=jnp.int32)[None, :]).astype(jnp.float32)
    return jnp.dot(matches, distance_mask.astype(jnp.float32), precision=lax.Precision.HIGHEST)

def cross_spectrum(row_slab, col_slab):
    bin_count = row_slab.shape[-1] // 2
    row_float = row_slab.astype(jnp.float32)
    col_float = col_slab.astype(jnp.float32)
    row_real, row_imag = (row_float[..., :bin_count], row_float[..., bin_count:])
    col_real, col_imag = (col_float[..., :bin_count], col_float[..., bin_count:])
    real_part = jnp.einsum('sif,sjf->ijf', row_real, col_real) + jnp.einsum('sif,sjf->ijf', row_imag, col_imag)
    imag_part = jnp.einsum('sif,sjf->ijf', row_real, col_imag) - jnp.einsum('sif,sjf->ijf', row_imag, col_real)
    return jnp.concatenate([real_part, imag_part], -1)

def reference(spectra, pair_lists, distance_mask):
    row_width = spectra.shape[-1]
    blocks = spectra.reshape(SEGS, N_PAIR, CB, row_width).transpose(1, 0, 2, 3)
    whitened = lax.map(whiten, blocks)
    lag_table = lag_weights(F, LAGS)
    scale_norm = 1.0 / math.sqrt(SEGS * F)

    def one_slot(slot_entry):
        row_block = slot_entry[0]
        col_block = slot_entry[1]
        is_live = (row_block >= 0).astype(jnp.float32)
        row_slab = lax.dynamic_index_in_dim(whitened, jnp.maximum(row_block, 0).astype(jnp.int32), 0, keepdims=False)
        col_slab = lax.dynamic_index_in_dim(whitened, jnp.maximum(col_block, 0).astype(jnp.int32), 0, keepdims=False)
        row_groups = row_slab.reshape(N_SEG, SEG_DEV, CB, row_width)
        col_groups = col_slab.reshape(N_SEG, SEG_DEV, CB, row_width)

        def add_group(running, group_slabs):
            partial_value = cross_spectrum(group_slabs[0], group_slabs[1]).astype(jnp.bfloat16)
            partial_value = lax.optimization_barrier(partial_value)
            return (running + partial_value.astype(jnp.float32), None)
        stacked = lax.scan(add_group, jnp.zeros((CB, CB, row_width), jnp.float32), (row_groups, col_groups))[0]
        stacked = stacked.astype(jnp.bfloat16)
        lagged = jnp.dot(stacked.reshape(CB * CB, row_width), lag_table, preferred_element_type=jnp.float32)
        factor = distance_factor(distance_mask, 0, CB, col_block - row_block, CB) * scale_norm * is_live
        return (lagged * factor[:, None]).astype(jnp.bfloat16).reshape(CB, CB, LAGS)
    flat_lists = pair_lists.reshape(N_PAIR * SLOTS, 2)
    result = lax.map(one_slot, flat_lists)
    return result.reshape(N_PAIR, SLOTS, CB, CB, LAGS)
```

```python
import math

import jax
import jax.numpy as jnp
from jax import lax
from jax.sharding import PartitionSpec as P

LAGS = 1025
SAMPLES = 6000
FIRST_BIN = 30
SMOOTH = 4
BAND_BLOCKS = 4
SLOTS = 2
NEAR_BINS = 2


def rotated(array, axis, by):
    peers = lax.axis_size(axis)
    pairs = [(i, (i + by) % peers) for i in range(peers)]
    return lax.ppermute(array, axis, pairs)


def whiten(spectra):
    bin_count = spectra.shape[-1] // 2
    as_float = spectra.astype(jnp.float32)
    real_part = as_float[..., :bin_count]
    imag_part = as_float[..., bin_count:]
    amplitude = jnp.sqrt(real_part * real_part + imag_part * imag_part + 1e-06)
    positions = jnp.arange(bin_count, dtype=jnp.int32)
    inside = (jnp.abs(positions[:, None] - positions[None, :]) <= SMOOTH).astype(jnp.float32)
    smoothing = inside / jnp.sum(inside, axis=0, keepdims=True)
    smoothed = jnp.matmul(amplitude, smoothing, precision=lax.Precision.HIGHEST)
    return jnp.concatenate([real_part / smoothed, imag_part / smoothed], -1).astype(jnp.bfloat16)


def lag_weights(bin_count, lag_count):
    frequency = jnp.arange(bin_count, dtype=jnp.int32) + FIRST_BIN
    lag_index = jnp.arange(lag_count, dtype=jnp.int32) - lag_count // 2
    phase_index = frequency[:, None] * lag_index[None, :] % SAMPLES
    theta = phase_index.astype(jnp.float32) * (2.0 * math.pi / SAMPLES)
    return jnp.concatenate([jnp.cos(theta), -jnp.sin(theta)], 0).astype(jnp.bfloat16)


def distance_factor(distance_mask, row_first, row_total, block_gap, col_total):
    row_ids = row_first + jnp.arange(row_total, dtype=jnp.int32)
    col_ids = jnp.arange(col_total, dtype=jnp.int32)
    distance = jnp.abs(col_total * block_gap + col_ids[None, :] - row_ids[:, None]).reshape(-1)
    matches = (
        distance[:, None] == jnp.arange(distance_mask.shape[0], dtype=jnp.int32)[None, :]
    ).astype(jnp.float32)
    return jnp.dot(matches, distance_mask.astype(jnp.float32), precision=lax.Precision.HIGHEST)


def cross_bins(row_slab, col_slab):
    bins, _, seg_total, channels = row_slab.shape
    row_both = row_slab.reshape(bins, 2 * seg_total, channels)
    col_both = col_slab.reshape(bins, 2 * seg_total, channels)
    row_sign = jnp.concatenate([row_slab[:, 0], -row_slab[:, 1]], 1)
    col_swap = jnp.concatenate([col_slab[:, 1], col_slab[:, 0]], 1)
    real_part = jnp.einsum("fsi,fsj->fij", row_both, col_both, preferred_element_type=jnp.float32)
    imag_part = jnp.einsum("fsi,fsj->fij", row_sign, col_swap, preferred_element_type=jnp.float32)
    return jnp.stack([real_part, imag_part], 1).astype(jnp.bfloat16)


def band_window(part, site_offset):
    pieces = {0: part}
    moving = part
    for d in range(1, site_offset + 1):
        moving = rotated(moving, "pair", 1)
        pieces[-d] = moving
    moving = part
    for d in range(1, BAND_BLOCKS - site_offset):
        moving = rotated(moving, "pair", -1)
        pieces[d] = moving
    return jnp.stack([pieces[d - site_offset] for d in range(BAND_BLOCKS)], 0)


def site_stack(part, pair_lists, site_offset):
    peers = lax.axis_size("pair")
    nearby = band_window(part, site_offset)
    owner_lists = rotated(pair_lists, "pair", site_offset)[0]
    owner = (lax.axis_index("pair") - site_offset) % peers
    per_slot = []
    for slot_index in range(SLOTS):
        row_offset = jnp.clip(owner_lists[slot_index, 0] - owner, 0, BAND_BLOCKS - 1)
        col_offset = jnp.clip(owner_lists[slot_index, 1] - owner, 0, BAND_BLOCKS - 1)
        row_slab = lax.dynamic_index_in_dim(nearby, row_offset, 0, keepdims=False)
        col_slab = lax.dynamic_index_in_dim(nearby, col_offset, 0, keepdims=False)
        per_slot.append(cross_bins(row_slab, col_slab))
    return rotated(jnp.stack(per_slot, 0), "pair", -site_offset)


def body(spectra, pair_lists, distance_mask):
    group_total = lax.axis_size("seg")
    seg_index = lax.axis_index("seg")
    seg_local, block_width, row_width = spectra.shape
    bin_count = row_width // 2
    group_bins = bin_count // group_total
    row_share = block_width // group_total

    whitened = whiten(spectra)
    by_bins = whitened.reshape(seg_local, block_width, 2, group_total, group_bins)
    by_bins = by_bins.transpose(3, 4, 2, 0, 1)
    by_bins = lax.all_to_all(by_bins, "seg", 0, 3, tiled=True)[0]

    near = site_stack(by_bins[:NEAR_BINS], pair_lists, 1)
    far = site_stack(by_bins[NEAR_BINS:], pair_lists, 2)
    stacked_bins = jnp.concatenate([near, far], 1)
    stacked_bins = stacked_bins.reshape(
        SLOTS, group_bins, 2, group_total, row_share, block_width
    )
    stacked_bins = lax.all_to_all(stacked_bins, "seg", 3, 3, tiled=True)
    stacked_all = stacked_bins.transpose(0, 4, 5, 2, 3, 1).reshape(
        SLOTS, row_share, block_width, row_width
    )

    lag_table = lag_weights(bin_count, LAGS)
    scale_norm = 1.0 / math.sqrt(seg_local * group_total * bin_count)
    outputs = []
    for slot_index in range(SLOTS):
        row_block = pair_lists[0, slot_index, 0]
        col_block = pair_lists[0, slot_index, 1]
        is_live = (row_block >= 0).astype(jnp.float32)
        lagged = jnp.dot(
            stacked_all[slot_index].reshape(-1, row_width),
            lag_table,
            preferred_element_type=jnp.float32,
        )
        factor = (
            distance_factor(
                distance_mask, seg_index * row_share, row_share, col_block - row_block, block_width
            )
            * scale_norm
            * is_live
        )
        outputs.append(
            (lagged * factor[:, None]).astype(jnp.bfloat16).reshape(row_share, block_width, LAGS)
        )
    return jnp.stack(outputs, 0)[None]


def solution(mesh):
    in_specs = (P("seg", "pair", None), P("pair", None, None), P())
    out_specs = P("pair", None, "seg", None, None)
    return jax.shard_map(body, mesh=mesh, in_specs=in_specs, out_specs=out_specs, check_vma=False)
```

```python
import math

import jax
import jax.numpy as jnp
from jax import lax
from jax.sharding import PartitionSpec as P

LAGS = 1025
SAMPLES = 6000
FIRST_BIN = 30
SMOOTH = 4
BAND_BLOCKS = 4
SLOTS = 2
NEAR_BINS = 2
SEG_CHUNKS = 2


def rotated(array, axis, by):
    peers = lax.axis_size(axis)
    pairs = [(i, (i + by) % peers) for i in range(peers)]
    return lax.ppermute(array, axis, pairs)


def whiten(spectra):
    bin_count = spectra.shape[-1] // 2
    as_float = spectra.astype(jnp.float32)
    real_part = as_float[..., :bin_count]
    imag_part = as_float[..., bin_count:]
    amplitude = jnp.sqrt(real_part * real_part + imag_part * imag_part + 1e-06)
    positions = jnp.arange(bin_count, dtype=jnp.int32)
    inside = (jnp.abs(positions[:, None] - positions[None, :]) <= SMOOTH).astype(jnp.float32)
    smoothing = inside / jnp.sum(inside, axis=0, keepdims=True)
    smoothed = jnp.matmul(amplitude, smoothing, precision=lax.Precision.HIGHEST)
    return jnp.concatenate([real_part / smoothed, imag_part / smoothed], -1).astype(jnp.bfloat16)


def lag_weights(bin_count, lag_count):
    frequency = jnp.arange(bin_count, dtype=jnp.int32) + FIRST_BIN
    lag_index = jnp.arange(lag_count, dtype=jnp.int32) - lag_count // 2
    phase_index = frequency[:, None] * lag_index[None, :] % SAMPLES
    theta = phase_index.astype(jnp.float32) * (2.0 * math.pi / SAMPLES)
    return jnp.concatenate([jnp.cos(theta), -jnp.sin(theta)], 0).astype(jnp.bfloat16)


def distance_factor(distance_mask, row_first, row_total, block_gap, col_total):
    row_ids = row_first + jnp.arange(row_total, dtype=jnp.int32)
    col_ids = jnp.arange(col_total, dtype=jnp.int32)
    distance = jnp.abs(col_total * block_gap + col_ids[None, :] - row_ids[:, None]).reshape(-1)
    matches = (
        distance[:, None] == jnp.arange(distance_mask.shape[0], dtype=jnp.int32)[None, :]
    ).astype(jnp.float32)
    return jnp.dot(matches, distance_mask.astype(jnp.float32), precision=lax.Precision.HIGHEST)


def cross_bins(row_slab, col_slab):
    bins, _, seg_total, channels = row_slab.shape
    row_both = row_slab.reshape(bins, 2 * seg_total, channels)
    col_both = col_slab.reshape(bins, 2 * seg_total, channels)
    row_sign = jnp.concatenate([row_slab[:, 0], -row_slab[:, 1]], 1)
    col_swap = jnp.concatenate([col_slab[:, 1], col_slab[:, 0]], 1)
    real_part = jnp.einsum("fsi,fsj->fij", row_both, col_both, preferred_element_type=jnp.float32)
    imag_part = jnp.einsum("fsi,fsj->fij", row_sign, col_swap, preferred_element_type=jnp.float32)
    return jnp.stack([real_part, imag_part], 1)


def band_window(part, site_offset):
    pieces = {0: part}
    moving = part
    for d in range(1, site_offset + 1):
        moving = rotated(moving, "pair", 1)
        pieces[-d] = moving
    moving = part
    for d in range(1, BAND_BLOCKS - site_offset):
        moving = rotated(moving, "pair", -1)
        pieces[d] = moving
    return jnp.stack([pieces[d - site_offset] for d in range(BAND_BLOCKS)], 0)


def site_stack(parts, pair_lists, site_offset):
    peers = lax.axis_size("pair")
    owner_lists = rotated(pair_lists, "pair", site_offset)[0]
    owner = (lax.axis_index("pair") - site_offset) % peers
    offsets = [
        (
            jnp.clip(owner_lists[slot_index, 0] - owner, 0, BAND_BLOCKS - 1),
            jnp.clip(owner_lists[slot_index, 1] - owner, 0, BAND_BLOCKS - 1),
        )
        for slot_index in range(SLOTS)
    ]
    totals = [None] * SLOTS
    for part in parts:
        nearby = band_window(part, site_offset)
        for slot_index in range(SLOTS):
            row_offset, col_offset = offsets[slot_index]
            row_slab = lax.dynamic_index_in_dim(nearby, row_offset, 0, keepdims=False)
            col_slab = lax.dynamic_index_in_dim(nearby, col_offset, 0, keepdims=False)
            term = cross_bins(row_slab, col_slab)
            totals[slot_index] = term if totals[slot_index] is None else totals[slot_index] + term
    stacked = jnp.stack(totals, 0).astype(jnp.bfloat16)
    return rotated(stacked, "pair", -site_offset)


def body(spectra, pair_lists, distance_mask):
    group_total = lax.axis_size("seg")
    seg_index = lax.axis_index("seg")
    seg_local, block_width, row_width = spectra.shape
    bin_count = row_width // 2
    group_bins = bin_count // group_total
    row_share = block_width // group_total

    whitened = whiten(spectra)
    chunk = seg_local // SEG_CHUNKS
    parts = []
    for chunk_index in range(SEG_CHUNKS):
        piece = whitened[chunk_index * chunk : (chunk_index + 1) * chunk]
        by_bins = piece.reshape(chunk, block_width, 2, group_total, group_bins)
        by_bins = by_bins.transpose(3, 4, 2, 0, 1)
        parts.append(lax.all_to_all(by_bins, "seg", 0, 3, tiled=True)[0])

    near = site_stack([part[:NEAR_BINS] for part in parts], pair_lists, 1)
    far = site_stack([part[NEAR_BINS:] for part in parts], pair_lists, 2)
    stacked_bins = jnp.concatenate([near, far], 1)
    stacked_bins = stacked_bins.reshape(
        SLOTS, group_bins, 2, group_total, row_share, block_width
    )
    stacked_bins = lax.all_to_all(stacked_bins, "seg", 3, 3, tiled=True)
    stacked_all = stacked_bins.transpose(0, 4, 5, 2, 3, 1).reshape(
        SLOTS, row_share, block_width, row_width
    )

    lag_table = lag_weights(bin_count, LAGS)
    scale_norm = 1.0 / math.sqrt(seg_local * group_total * bin_count)
    outputs = []
    for slot_index in range(SLOTS):
        row_block = pair_lists[0, slot_index, 0]
        col_block = pair_lists[0, slot_index, 1]
        is_live = (row_block >= 0).astype(jnp.float32)
        lagged = jnp.dot(
            stacked_all[slot_index].reshape(-1, row_width),
            lag_table,
            preferred_element_type=jnp.float32,
        )
        factor = (
            distance_factor(
                distance_mask, seg_index * row_share, row_share, col_block - row_block, block_width
            )
            * scale_norm
            * is_live
        )
        outputs.append(
            (lagged * factor[:, None]).astype(jnp.bfloat16).reshape(row_share, block_width, LAGS)
        )
    return jnp.stack(outputs, 0)[None]


def solution(mesh):
    in_specs = (P("seg", "pair", None), P("pair", None, None), P())
    out_specs = P("pair", None, "seg", None, None)
    return jax.shard_map(body, mesh=mesh, in_specs=in_specs, out_specs=out_specs, check_vma=False)
```

```python
import functools
import math

import jax
import jax.numpy as jnp
from jax import lax
from jax.experimental import pallas as pl
from jax.experimental.pallas import tpu as pltpu
from jax.sharding import PartitionSpec as P

LAGS = 1025
SAMPLES = 6000
FIRST_BIN = 30
SMOOTH = 4
BAND_BLOCKS = 4
SLOTS = 2
NEAR_BINS = 2


def rotated(array, axis, by):
    peers = lax.axis_size(axis)
    pairs = [(i, (i + by) % peers) for i in range(peers)]
    return lax.ppermute(array, axis, pairs)


def whiten(spectra):
    bin_count = spectra.shape[-1] // 2
    as_float = spectra.astype(jnp.float32)
    real_part = as_float[..., :bin_count]
    imag_part = as_float[..., bin_count:]
    amplitude = jnp.sqrt(real_part * real_part + imag_part * imag_part + 1e-06)
    positions = jnp.arange(bin_count, dtype=jnp.int32)
    inside = (jnp.abs(positions[:, None] - positions[None, :]) <= SMOOTH).astype(jnp.float32)
    smoothing = inside / jnp.sum(inside, axis=0, keepdims=True)
    smoothed = jnp.matmul(amplitude, smoothing, precision=lax.Precision.HIGHEST)
    return jnp.concatenate([real_part / smoothed, imag_part / smoothed], -1).astype(jnp.bfloat16)


def lag_weights(bin_count, lag_count):
    frequency = jnp.arange(bin_count, dtype=jnp.int32) + FIRST_BIN
    lag_index = jnp.arange(lag_count, dtype=jnp.int32) - lag_count // 2
    phase_index = frequency[:, None] * lag_index[None, :] % SAMPLES
    theta = phase_index.astype(jnp.float32) * (2.0 * math.pi / SAMPLES)
    return jnp.concatenate([jnp.cos(theta), -jnp.sin(theta)], 0).astype(jnp.bfloat16)


def distance_factor(distance_mask, row_first, row_total, block_gap, col_total):
    row_ids = row_first + jnp.arange(row_total, dtype=jnp.int32)
    col_ids = jnp.arange(col_total, dtype=jnp.int32)
    distance = jnp.abs(col_total * block_gap + col_ids[None, :] - row_ids[:, None]).reshape(-1)
    matches = (
        distance[:, None] == jnp.arange(distance_mask.shape[0], dtype=jnp.int32)[None, :]
    ).astype(jnp.float32)
    return jnp.dot(matches, distance_mask.astype(jnp.float32), precision=lax.Precision.HIGHEST)


def cross_kernel(bin_starts, offsets_ref, *refs):
    pieces = refs[:BAND_BLOCKS]
    out_ref, row_buf, col_buf, sems = refs[BAND_BLOCKS:]
    bins = row_buf.shape[1]
    for slot_index in range(SLOTS):
        for side, buf in ((0, row_buf), (1, col_buf)):
            index = offsets_ref[slot_index, side]
            for d in range(BAND_BLOCKS):

                @pl.when(index == d)
                def _start(d=d, buf=buf, side=side):
                    source = pieces[d].at[pl.ds(bin_starts[d], bins)]
                    pltpu.make_async_copy(
                        source, buf.at[slot_index], sems.at[slot_index, side]
                    ).start()

    nt = (((1,), (1,)), ((), ()))

    def dot(a, b):
        return lax.dot_general(a, b, nt, preferred_element_type=jnp.float32)

    for slot_index in range(SLOTS):
        for side, buf in ((0, row_buf), (1, col_buf)):
            source = pieces[0].at[pl.ds(bin_starts[0], bins)]
            pltpu.make_async_copy(source, buf.at[slot_index], sems.at[slot_index, side]).wait()

        def per_bin(f, carry, slot_index=slot_index):
            row_re = row_buf[slot_index, f, 0]
            row_im = row_buf[slot_index, f, 1]
            col_re = col_buf[slot_index, f, 0]
            col_im = col_buf[slot_index, f, 1]
            real_part = dot(row_re, col_re) + dot(row_im, col_im)
            imag_part = dot(row_re, col_im) - dot(row_im, col_re)
            out_ref[slot_index, f, 0] = real_part.astype(out_ref.dtype)
            out_ref[slot_index, f, 1] = imag_part.astype(out_ref.dtype)
            return carry

        lax.fori_loop(0, bins, per_bin, 0)


def cross_slots(offsets, pieces, bin_starts, bins):
    _, _, channels, seg_total = pieces[0].shape
    buffer = pltpu.VMEM((SLOTS, bins, 2, channels, seg_total), jnp.bfloat16)
    return pl.pallas_call(
        functools.partial(cross_kernel, tuple(bin_starts)),
        out_shape=jax.ShapeDtypeStruct((SLOTS, bins, 2, channels, channels), jnp.bfloat16),
        in_specs=[pl.BlockSpec(memory_space=pltpu.SMEM)]
        + [pl.BlockSpec(memory_space=pl.ANY)] * BAND_BLOCKS,
        out_specs=pl.BlockSpec(memory_space=pltpu.VMEM),
        scratch_shapes=[buffer, buffer, pltpu.SemaphoreType.DMA((SLOTS, 2))],
    )(offsets, *pieces)


def site_stack(pieces, bin_starts, bins, pair_lists, site_offset):
    peers = lax.axis_size("pair")
    owner_lists = rotated(pair_lists, "pair", site_offset)[0]
    owner = (lax.axis_index("pair") - site_offset) % peers
    offsets = jnp.clip(owner_lists - owner, 0, BAND_BLOCKS - 1).astype(jnp.int32)
    stacked = cross_slots(offsets, pieces, bin_starts, bins)
    return rotated(stacked, "pair", -site_offset)


def body(spectra, pair_lists, distance_mask):
    group_total = lax.axis_size("seg")
    seg_index = lax.axis_index("seg")
    seg_local, block_width, row_width = spectra.shape
    bin_count = row_width // 2
    group_bins = bin_count // group_total
    row_share = block_width // group_total

    whitened = whiten(spectra)
    by_bins = whitened.reshape(seg_local, block_width, 2, group_total, group_bins)
    by_bins = by_bins.transpose(3, 4, 2, 1, 0)
    by_bins = lax.all_to_all(by_bins, "seg", 0, 4, tiled=True)[0]

    from_below = rotated(by_bins, "pair", 1)
    from_above = rotated(by_bins, "pair", -1)
    two_below = rotated(from_below[NEAR_BINS:], "pair", 1)
    two_above = rotated(from_above[:NEAR_BINS], "pair", -1)
    far_bins = group_bins - NEAR_BINS
    near = site_stack(
        (from_below, by_bins, from_above, two_above), (0, 0, 0, 0), NEAR_BINS, pair_lists, 1
    )
    far = site_stack(
        (two_below, from_below, by_bins, from_above),
        (0, NEAR_BINS, NEAR_BINS, NEAR_BINS),
        far_bins,
        pair_lists,
        2,
    )
    stacked_bins = jnp.concatenate([near, far], 1)
    stacked_bins = stacked_bins.reshape(
        SLOTS, group_bins, 2, group_total, row_share, block_width
    )
    stacked_bins = lax.all_to_all(stacked_bins, "seg", 3, 3, tiled=True)
    stacked_all = stacked_bins.transpose(0, 4, 5, 2, 3, 1).reshape(
        SLOTS, row_share, block_width, row_width
    )

    lag_table = lag_weights(bin_count, LAGS)
    scale_norm = 1.0 / math.sqrt(seg_local * group_total * bin_count)
    outputs = []
    for slot_index in range(SLOTS):
        row_block = pair_lists[0, slot_index, 0]
        col_block = pair_lists[0, slot_index, 1]
        is_live = (row_block >= 0).astype(jnp.float32)
        lagged = jnp.dot(
            stacked_all[slot_index].reshape(-1, row_width),
            lag_table,
            preferred_element_type=jnp.float32,
        )
        factor = (
            distance_factor(
                distance_mask, seg_index * row_share, row_share, col_block - row_block, block_width
            )
            * scale_norm
            * is_live
        )
        outputs.append(
            (lagged * factor[:, None]).astype(jnp.bfloat16).reshape(row_share, block_width, LAGS)
        )
    return jnp.stack(outputs, 0)[None]


def solution(mesh):
    in_specs = (P("seg", "pair", None), P("pair", None, None), P())
    out_specs = P("pair", None, "seg", None, None)
    return jax.shard_map(body, mesh=mesh, in_specs=in_specs, out_specs=out_specs, check_vma=False)
```

```python
import functools
import math

import jax
import jax.numpy as jnp
from jax import lax
from jax.experimental import pallas as pl
from jax.experimental.pallas import tpu as pltpu
from jax.sharding import PartitionSpec as P

LAGS = 1025
SAMPLES = 6000
FIRST_BIN = 30
SMOOTH = 4
BAND_BLOCKS = 4
SLOTS = 2
NEAR_BINS = 2


def rotated(array, axis, by):
    peers = lax.axis_size(axis)
    pairs = [(i, (i + by) % peers) for i in range(peers)]
    return lax.ppermute(array, axis, pairs)


def whiten(spectra):
    bin_count = spectra.shape[-1] // 2
    as_float = spectra.astype(jnp.float32)
    real_part = as_float[..., :bin_count]
    imag_part = as_float[..., bin_count:]
    amplitude = jnp.sqrt(real_part * real_part + imag_part * imag_part + 1e-06)
    positions = jnp.arange(bin_count, dtype=jnp.int32)
    inside = (jnp.abs(positions[:, None] - positions[None, :]) <= SMOOTH).astype(jnp.float32)
    smoothing = inside / jnp.sum(inside, axis=0, keepdims=True)
    smoothed = jnp.matmul(amplitude, smoothing, precision=lax.Precision.HIGHEST)
    return jnp.concatenate([real_part / smoothed, imag_part / smoothed], -1).astype(jnp.bfloat16)


def lag_weights(bin_count, lag_count):
    frequency = jnp.arange(bin_count, dtype=jnp.int32) + FIRST_BIN
    lag_index = jnp.arange(lag_count, dtype=jnp.int32) - lag_count // 2
    phase_index = frequency[:, None] * lag_index[None, :] % SAMPLES
    theta = phase_index.astype(jnp.float32) * (2.0 * math.pi / SAMPLES)
    return jnp.concatenate([jnp.cos(theta), -jnp.sin(theta)], 0).astype(jnp.bfloat16)


def distance_factor(distance_mask, row_first, row_total, block_gap, col_total):
    row_ids = row_first + jnp.arange(row_total, dtype=jnp.int32)
    col_ids = jnp.arange(col_total, dtype=jnp.int32)
    distance = jnp.abs(col_total * block_gap + col_ids[None, :] - row_ids[:, None]).reshape(-1)
    matches = (
        distance[:, None] == jnp.arange(distance_mask.shape[0], dtype=jnp.int32)[None, :]
    ).astype(jnp.float32)
    return jnp.dot(matches, distance_mask.astype(jnp.float32), precision=lax.Precision.HIGHEST)


def cross_kernel(bin_starts, offsets_ref, *refs):
    pieces = refs[:BAND_BLOCKS]
    out_ref, row_buf, col_buf, sems = refs[BAND_BLOCKS:]
    bins = row_buf.shape[1]
    for slot_index in range(SLOTS):
        for side, buf in ((0, row_buf), (1, col_buf)):
            index = offsets_ref[slot_index, side]
            for d in range(BAND_BLOCKS):

                @pl.when(index == d)
                def _start(d=d, buf=buf, side=side):
                    source = pieces[d].at[pl.ds(bin_starts[d], bins)]
                    pltpu.make_async_copy(
                        source, buf.at[slot_index], sems.at[slot_index, side]
                    ).start()

    nt = (((1,), (1,)), ((), ()))

    def dot(a, b):
        return lax.dot_general(a, b, nt, preferred_element_type=jnp.float32)

    for slot_index in range(SLOTS):
        for side, buf in ((0, row_buf), (1, col_buf)):
            source = pieces[0].at[pl.ds(bin_starts[0], bins)]
            pltpu.make_async_copy(source, buf.at[slot_index], sems.at[slot_index, side]).wait()

        def per_bin(f, carry, slot_index=slot_index):
            row_re = row_buf[slot_index, f, 0]
            row_im = row_buf[slot_index, f, 1]
            col_re = col_buf[slot_index, f, 0]
            col_im = col_buf[slot_index, f, 1]
            real_part = dot(row_re, col_re) + dot(row_im, col_im)
            imag_part = dot(row_re, col_im) - dot(row_im, col_re)
            out_ref[slot_index, f, 0] = real_part.astype(out_ref.dtype)
            out_ref[slot_index, f, 1] = imag_part.astype(out_ref.dtype)
            return carry

        lax.fori_loop(0, bins, per_bin, 0)


def cross_slots(offsets, pieces, bin_starts, bins):
    _, _, channels, seg_total = pieces[0].shape
    buffer = pltpu.VMEM((SLOTS, bins, 2, channels, seg_total), jnp.bfloat16)
    return pl.pallas_call(
        functools.partial(cross_kernel, tuple(bin_starts)),
        out_shape=jax.ShapeDtypeStruct((SLOTS, bins, 2, channels, channels), jnp.bfloat16),
        in_specs=[pl.BlockSpec(memory_space=pltpu.SMEM)]
        + [pl.BlockSpec(memory_space=pl.ANY)] * BAND_BLOCKS,
        out_specs=pl.BlockSpec(memory_space=pltpu.VMEM),
        scratch_shapes=[buffer, buffer, pltpu.SemaphoreType.DMA((SLOTS, 2))],
    )(offsets, *pieces)


def site_stack(pieces, bin_starts, bins, pair_lists, site_offset):
    peers = lax.axis_size("pair")
    owner_lists = rotated(pair_lists, "pair", site_offset)[0]
    owner = (lax.axis_index("pair") - site_offset) % peers
    offsets = jnp.clip(owner_lists - owner, 0, BAND_BLOCKS - 1).astype(jnp.int32)
    stacked = cross_slots(offsets, pieces, bin_starts, bins)
    return rotated(stacked, "pair", -site_offset)


def body(spectra, pair_lists, distance_mask):
    group_total = lax.axis_size("seg")
    seg_index = lax.axis_index("seg")
    seg_local, block_width, row_width = spectra.shape
    bin_count = row_width // 2
    group_bins = bin_count // group_total
    row_share = block_width // group_total

    whitened = whiten(spectra)
    by_bins = whitened.reshape(seg_local, block_width, 2, group_total, group_bins)
    by_bins = by_bins.transpose(3, 4, 2, 1, 0)
    far_local = lax.all_to_all(by_bins[:, NEAR_BINS:], "seg", 0, 4, tiled=True)[0]
    near_local = lax.all_to_all(by_bins[:, :NEAR_BINS], "seg", 0, 4, tiled=True)[0]

    far_below = rotated(far_local, "pair", 1)
    far_above = rotated(far_local, "pair", -1)
    far_two_below = rotated(far_below, "pair", 1)
    near_below = rotated(near_local, "pair", 1)
    near_above = rotated(near_local, "pair", -1)
    near_two_above = rotated(near_above, "pair", -1)
    far_bins = group_bins - NEAR_BINS
    far = site_stack(
        (far_two_below, far_below, far_local, far_above), (0, 0, 0, 0), far_bins, pair_lists, 2
    )
    near = site_stack(
        (near_below, near_local, near_above, near_two_above), (0, 0, 0, 0), NEAR_BINS, pair_lists, 1
    )
    stacked_bins = jnp.concatenate([near, far], 1)
    stacked_bins = stacked_bins.reshape(
        SLOTS, group_bins, 2, group_total, row_share, block_width
    )
    stacked_bins = lax.all_to_all(stacked_bins, "seg", 3, 3, tiled=True)
    stacked_all = stacked_bins.transpose(0, 4, 5, 2, 3, 1).reshape(
        SLOTS, row_share, block_width, row_width
    )

    lag_table = lag_weights(bin_count, LAGS)
    scale_norm = 1.0 / math.sqrt(seg_local * group_total * bin_count)
    lagged = jnp.dot(
        stacked_all.reshape(-1, row_width), lag_table, preferred_element_type=jnp.float32
    )
    factors = []
    for slot_index in range(SLOTS):
        row_block = pair_lists[0, slot_index, 0]
        col_block = pair_lists[0, slot_index, 1]
        is_live = (row_block >= 0).astype(jnp.float32)
        factors.append(
            distance_factor(
                distance_mask, seg_index * row_share, row_share, col_block - row_block, block_width
            )
            * scale_norm
            * is_live
        )
    factor = jnp.concatenate(factors, 0)
    correlations = (lagged * factor[:, None]).astype(jnp.bfloat16)
    return correlations.reshape(1, SLOTS, row_share, block_width, LAGS)


def solution(mesh):
    in_specs = (P("seg", "pair", None), P("pair", None, None), P())
    out_specs = P("pair", None, "seg", None, None)
    return jax.shard_map(body, mesh=mesh, in_specs=in_specs, out_specs=out_specs, check_vma=False)
```

```python
import functools
import math

import jax
import jax.numpy as jnp
from jax import lax
from jax.experimental import pallas as pl
from jax.experimental.pallas import tpu as pltpu
from jax.sharding import PartitionSpec as P

LAGS = 1025
SAMPLES = 6000
FIRST_BIN = 30
SMOOTH = 4
BAND_BLOCKS = 4
SLOTS = 2
NEAR_BINS = 2


def rotated(array, axis, by):
    peers = lax.axis_size(axis)
    pairs = [(i, (i + by) % peers) for i in range(peers)]
    return lax.ppermute(array, axis, pairs)


def whiten(spectra):
    bin_count = spectra.shape[-1] // 2
    as_float = spectra.astype(jnp.float32)
    real_part = as_float[..., :bin_count]
    imag_part = as_float[..., bin_count:]
    amplitude = jnp.sqrt(real_part * real_part + imag_part * imag_part + 1e-06)
    positions = jnp.arange(bin_count, dtype=jnp.int32)
    inside = (jnp.abs(positions[:, None] - positions[None, :]) <= SMOOTH).astype(jnp.float32)
    smoothing = inside / jnp.sum(inside, axis=0, keepdims=True)
    smoothed = jnp.matmul(amplitude, smoothing, precision=lax.Precision.HIGHEST)
    return jnp.concatenate([real_part / smoothed, imag_part / smoothed], -1).astype(jnp.bfloat16)


def lag_weights(bin_count, lag_count):
    frequency = jnp.arange(bin_count, dtype=jnp.int32) + FIRST_BIN
    lag_index = jnp.arange(lag_count, dtype=jnp.int32) - lag_count // 2
    phase_index = frequency[:, None] * lag_index[None, :] % SAMPLES
    theta = phase_index.astype(jnp.float32) * (2.0 * math.pi / SAMPLES)
    return jnp.concatenate([jnp.cos(theta), -jnp.sin(theta)], 0).astype(jnp.bfloat16)


def distance_factor(distance_mask, row_first, row_total, block_gap, col_total):
    row_ids = row_first + jnp.arange(row_total, dtype=jnp.int32)
    col_ids = jnp.arange(col_total, dtype=jnp.int32)
    distance = jnp.abs(col_total * block_gap + col_ids[None, :] - row_ids[:, None]).reshape(-1)
    matches = (
        distance[:, None] == jnp.arange(distance_mask.shape[0], dtype=jnp.int32)[None, :]
    ).astype(jnp.float32)
    return jnp.dot(matches, distance_mask.astype(jnp.float32), precision=lax.Precision.HIGHEST)


def cross_kernel(bin_starts, offsets_ref, *refs):
    pieces = refs[:BAND_BLOCKS]
    out_ref, row_buf, col_buf, sems = refs[BAND_BLOCKS:]
    bins = row_buf.shape[1]
    for slot_index in range(SLOTS):
        for side, buf in ((0, row_buf), (1, col_buf)):
            index = offsets_ref[slot_index, side]
            for d in range(BAND_BLOCKS):

                @pl.when(index == d)
                def _start(d=d, buf=buf, side=side):
                    source = pieces[d].at[pl.ds(bin_starts[d], bins)]
                    pltpu.make_async_copy(
                        source, buf.at[slot_index], sems.at[slot_index, side]
                    ).start()

    nt = (((1,), (1,)), ((), ()))

    def dot(a, b):
        return lax.dot_general(a, b, nt, preferred_element_type=jnp.float32)

    for slot_index in range(SLOTS):
        for side, buf in ((0, row_buf), (1, col_buf)):
            source = pieces[0].at[pl.ds(bin_starts[0], bins)]
            pltpu.make_async_copy(source, buf.at[slot_index], sems.at[slot_index, side]).wait()

        def per_bin(f, carry, slot_index=slot_index):
            row_re = row_buf[slot_index, f, 0]
            row_im = row_buf[slot_index, f, 1]
            col_re = col_buf[slot_index, f, 0]
            col_im = col_buf[slot_index, f, 1]
            real_part = dot(row_re, col_re) + dot(row_im, col_im)
            imag_part = dot(row_re, col_im) - dot(row_im, col_re)
            out_ref[slot_index, f, 0] = real_part.astype(out_ref.dtype)
            out_ref[slot_index, f, 1] = imag_part.astype(out_ref.dtype)
            return carry

        lax.fori_loop(0, bins, per_bin, 0)


def cross_slots(offsets, pieces, bin_starts, bins):
    _, _, channels, seg_total = pieces[0].shape
    buffer = pltpu.VMEM((SLOTS, bins, 2, channels, seg_total), jnp.bfloat16)
    return pl.pallas_call(
        functools.partial(cross_kernel, tuple(bin_starts)),
        out_shape=jax.ShapeDtypeStruct((SLOTS, bins, 2, channels, channels), jnp.bfloat16),
        in_specs=[pl.BlockSpec(memory_space=pltpu.SMEM)]
        + [pl.BlockSpec(memory_space=pl.ANY)] * BAND_BLOCKS,
        out_specs=pl.BlockSpec(memory_space=pltpu.VMEM),
        scratch_shapes=[buffer, buffer, pltpu.SemaphoreType.DMA((SLOTS, 2))],
    )(offsets, *pieces)


def site_stack(pieces, bin_starts, bins, pair_lists, site_offset):
    peers = lax.axis_size("pair")
    owner_lists = rotated(pair_lists, "pair", site_offset)[0]
    owner = (lax.axis_index("pair") - site_offset) % peers
    offsets = jnp.clip(owner_lists - owner, 0, BAND_BLOCKS - 1).astype(jnp.int32)
    stacked = cross_slots(offsets, pieces, bin_starts, bins)
    return rotated(stacked, "pair", -site_offset)


def body(spectra, pair_lists, distance_mask):
    group_total = lax.axis_size("seg")
    seg_index = lax.axis_index("seg")
    seg_local, block_width, row_width = spectra.shape
    bin_count = row_width // 2
    group_bins = bin_count // group_total
    row_share = block_width // group_total

    whitened = whiten(spectra)
    by_bins = whitened.reshape(seg_local, block_width, 2, group_total, group_bins)
    by_bins = by_bins.transpose(3, 4, 2, 1, 0)
    far_local = lax.all_to_all(by_bins[:, NEAR_BINS:], "seg", 0, 4, tiled=True)[0]
    near_local = lax.all_to_all(by_bins[:, :NEAR_BINS], "seg", 0, 4, tiled=True)[0]

    far_below = rotated(far_local, "pair", 1)
    far_above = rotated(far_local, "pair", -1)
    far_two_below = rotated(far_below, "pair", 1)
    near_below = rotated(near_local, "pair", 1)
    near_above = rotated(near_local, "pair", -1)
    near_two_above = rotated(near_above, "pair", -1)
    far_bins = group_bins - NEAR_BINS
    far = site_stack(
        (far_two_below, far_below, far_local, far_above), (0, 0, 0, 0), far_bins, pair_lists, 2
    )
    near = site_stack(
        (near_below, near_local, near_above, near_two_above), (0, 0, 0, 0), NEAR_BINS, pair_lists, 1
    )
    stacked_bins = jnp.concatenate([near, far], 1)
    stacked_bins = stacked_bins.reshape(
        SLOTS, group_bins, 2, group_total, row_share, block_width
    )
    stacked_bins = lax.all_to_all(stacked_bins, "seg", 3, 3, tiled=True)
    stacked_all = stacked_bins.transpose(0, 4, 5, 2, 3, 1).reshape(
        SLOTS, row_share, block_width, row_width
    )

    lag_table = lag_weights(bin_count, LAGS)
    scale_norm = 1.0 / math.sqrt(seg_local * group_total * bin_count)
    outputs = []
    for slot_index in range(SLOTS):
        row_block = pair_lists[0, slot_index, 0]
        col_block = pair_lists[0, slot_index, 1]
        is_live = (row_block >= 0).astype(jnp.float32)
        lagged = jnp.dot(
            stacked_all[slot_index].reshape(-1, row_width),
            lag_table,
            preferred_element_type=jnp.float32,
        )
        factor = (
            distance_factor(
                distance_mask, seg_index * row_share, row_share, col_block - row_block, block_width
            )
            * scale_norm
            * is_live
        )
        outputs.append(
            (lagged * factor[:, None]).astype(jnp.bfloat16).reshape(row_share, block_width, LAGS)
        )
    return jnp.stack(outputs, 0)[None]


def solution(mesh):
    in_specs = (P("seg", "pair", None), P("pair", None, None), P())
    out_specs = P("pair", None, "seg", None, None)
    return jax.shard_map(body, mesh=mesh, in_specs=in_specs, out_specs=out_specs, check_vma=False)
```

```python
import functools
import math

import jax
import jax.numpy as jnp
from jax import lax
from jax.experimental import pallas as pl
from jax.experimental.pallas import tpu as pltpu
from jax.sharding import PartitionSpec as P

LAGS = 1025
SAMPLES = 6000
FIRST_BIN = 30
SMOOTH = 4
BAND_BLOCKS = 4
SLOTS = 2
NEAR_BINS = 3


def rotated(array, axis, by):
    peers = lax.axis_size(axis)
    pairs = [(i, (i + by) % peers) for i in range(peers)]
    return lax.ppermute(array, axis, pairs)


def whiten(spectra):
    bin_count = spectra.shape[-1] // 2
    as_float = spectra.astype(jnp.float32)
    real_part = as_float[..., :bin_count]
    imag_part = as_float[..., bin_count:]
    amplitude = jnp.sqrt(real_part * real_part + imag_part * imag_part + 1e-06)
    positions = jnp.arange(bin_count, dtype=jnp.int32)
    inside = (jnp.abs(positions[:, None] - positions[None, :]) <= SMOOTH).astype(jnp.float32)
    smoothing = inside / jnp.sum(inside, axis=0, keepdims=True)
    smoothed = jnp.matmul(amplitude, smoothing, precision=lax.Precision.HIGHEST)
    return jnp.concatenate([real_part / smoothed, imag_part / smoothed], -1).astype(jnp.bfloat16)


def lag_weights(bin_count, lag_count):
    frequency = jnp.arange(bin_count, dtype=jnp.int32) + FIRST_BIN
    lag_index = jnp.arange(lag_count, dtype=jnp.int32) - lag_count // 2
    phase_index = frequency[:, None] * lag_index[None, :] % SAMPLES
    theta = phase_index.astype(jnp.float32) * (2.0 * math.pi / SAMPLES)
    return jnp.concatenate([jnp.cos(theta), -jnp.sin(theta)], 0).astype(jnp.bfloat16)


def distance_factor(distance_mask, row_first, row_total, block_gap, col_total):
    row_ids = row_first + jnp.arange(row_total, dtype=jnp.int32)
    col_ids = jnp.arange(col_total, dtype=jnp.int32)
    distance = jnp.abs(col_total * block_gap + col_ids[None, :] - row_ids[:, None]).reshape(-1)
    matches = (
        distance[:, None] == jnp.arange(distance_mask.shape[0], dtype=jnp.int32)[None, :]
    ).astype(jnp.float32)
    return jnp.dot(matches, distance_mask.astype(jnp.float32), precision=lax.Precision.HIGHEST)


def cross_kernel(bin_starts, offsets_ref, *refs):
    pieces = refs[:BAND_BLOCKS]
    out_ref, row_buf, col_buf, sems = refs[BAND_BLOCKS:]
    bins = row_buf.shape[1]
    for slot_index in range(SLOTS):
        for side, buf in ((0, row_buf), (1, col_buf)):
            index = offsets_ref[slot_index, side]
            for d in range(BAND_BLOCKS):

                @pl.when(index == d)
                def _start(d=d, buf=buf, side=side):
                    source = pieces[d].at[pl.ds(bin_starts[d], bins)]
                    pltpu.make_async_copy(
                        source, buf.at[slot_index], sems.at[slot_index, side]
                    ).start()

    nt = (((1,), (1,)), ((), ()))

    def dot(a, b):
        return lax.dot_general(a, b, nt, preferred_element_type=jnp.float32)

    for slot_index in range(SLOTS):
        for side, buf in ((0, row_buf), (1, col_buf)):
            source = pieces[0].at[pl.ds(bin_starts[0], bins)]
            pltpu.make_async_copy(source, buf.at[slot_index], sems.at[slot_index, side]).wait()

        def per_bin(f, carry, slot_index=slot_index):
            row_re = row_buf[slot_index, f, 0]
            row_im = row_buf[slot_index, f, 1]
            col_re = col_buf[slot_index, f, 0]
            col_im = col_buf[slot_index, f, 1]
            real_part = dot(row_re, col_re) + dot(row_im, col_im)
            imag_part = dot(row_re, col_im) - dot(row_im, col_re)
            out_ref[slot_index, f, 0] = real_part.astype(out_ref.dtype)
            out_ref[slot_index, f, 1] = imag_part.astype(out_ref.dtype)
            return carry

        lax.fori_loop(0, bins, per_bin, 0)


def cross_slots(offsets, pieces, bin_starts, bins):
    _, _, channels, seg_total = pieces[0].shape
    buffer = pltpu.VMEM((SLOTS, bins, 2, channels, seg_total), jnp.bfloat16)
    return pl.pallas_call(
        functools.partial(cross_kernel, tuple(bin_starts)),
        out_shape=jax.ShapeDtypeStruct((SLOTS, bins, 2, channels, channels), jnp.bfloat16),
        in_specs=[pl.BlockSpec(memory_space=pltpu.SMEM)]
        + [pl.BlockSpec(memory_space=pl.ANY)] * BAND_BLOCKS,
        out_specs=pl.BlockSpec(memory_space=pltpu.VMEM),
        scratch_shapes=[buffer, buffer, pltpu.SemaphoreType.DMA((SLOTS, 2))],
    )(offsets, *pieces)


def site_stack(pieces, bin_starts, bins, pair_lists, site_offset):
    peers = lax.axis_size("pair")
    owner_lists = rotated(pair_lists, "pair", site_offset)[0]
    owner = (lax.axis_index("pair") - site_offset) % peers
    offsets = jnp.clip(owner_lists - owner, 0, BAND_BLOCKS - 1).astype(jnp.int32)
    stacked = cross_slots(offsets, pieces, bin_starts, bins)
    return rotated(stacked, "pair", -site_offset)


def body(spectra, pair_lists, distance_mask):
    group_total = lax.axis_size("seg")
    seg_index = lax.axis_index("seg")
    seg_local, block_width, row_width = spectra.shape
    bin_count = row_width // 2
    group_bins = bin_count // group_total
    row_share = block_width // group_total

    whitened = whiten(spectra)
    by_bins = whitened.reshape(seg_local, block_width, 2, group_total, group_bins)
    by_bins = by_bins.transpose(3, 4, 2, 1, 0)
    far_local = lax.all_to_all(by_bins[:, NEAR_BINS:], "seg", 0, 4, tiled=True)[0]
    near_local = lax.all_to_all(by_bins[:, :NEAR_BINS], "seg", 0, 4, tiled=True)[0]

    far_below = rotated(far_local, "pair", 1)
    far_above = rotated(far_local, "pair", -1)
    far_two_below = rotated(far_below, "pair", 1)
    near_below = rotated(near_local, "pair", 1)
    near_above = rotated(near_local, "pair", -1)
    near_two_above = rotated(near_above, "pair", -1)
    far_bins = group_bins - NEAR_BINS
    far = site_stack(
        (far_two_below, far_below, far_local, far_above), (0, 0, 0, 0), far_bins, pair_lists, 2
    )
    near = site_stack(
        (near_below, near_local, near_above, near_two_above), (0, 0, 0, 0), NEAR_BINS, pair_lists, 1
    )
    stacked_bins = jnp.concatenate([near, far], 1)
    stacked_bins = stacked_bins.reshape(
        SLOTS, group_bins, 2, group_total, row_share, block_width
    )
    stacked_bins = lax.all_to_all(stacked_bins, "seg", 3, 3, tiled=True)
    stacked_all = stacked_bins.transpose(0, 4, 5, 2, 3, 1).reshape(
        SLOTS, row_share, block_width, row_width
    )

    lag_table = lag_weights(bin_count, LAGS)
    scale_norm = 1.0 / math.sqrt(seg_local * group_total * bin_count)
    outputs = []
    for slot_index in range(SLOTS):
        row_block = pair_lists[0, slot_index, 0]
        col_block = pair_lists[0, slot_index, 1]
        is_live = (row_block >= 0).astype(jnp.float32)
        lagged = jnp.dot(
            stacked_all[slot_index].reshape(-1, row_width),
            lag_table,
            preferred_element_type=jnp.float32,
        )
        factor = (
            distance_factor(
                distance_mask, seg_index * row_share, row_share, col_block - row_block, block_width
            )
            * scale_norm
            * is_live
        )
        outputs.append(
            (lagged * factor[:, None]).astype(jnp.bfloat16).reshape(row_share, block_width, LAGS)
        )
    return jnp.stack(outputs, 0)[None]


def solution(mesh):
    in_specs = (P("seg", "pair", None), P("pair", None, None), P())
    out_specs = P("pair", None, "seg", None, None)
    return jax.shard_map(body, mesh=mesh, in_specs=in_specs, out_specs=out_specs, check_vma=False)
```

```python
import functools
import math

import jax
import jax.numpy as jnp
from jax import lax
from jax.experimental import pallas as pl
from jax.experimental.pallas import tpu as pltpu
from jax.sharding import PartitionSpec as P

LAGS = 1025
SAMPLES = 6000
FIRST_BIN = 30
SMOOTH = 4
BAND_BLOCKS = 4
SLOTS = 2
NEAR_BINS = 4


def rotated(array, axis, by):
    peers = lax.axis_size(axis)
    pairs = [(i, (i + by) % peers) for i in range(peers)]
    return lax.ppermute(array, axis, pairs)


def whiten(spectra):
    bin_count = spectra.shape[-1] // 2
    as_float = spectra.astype(jnp.float32)
    real_part = as_float[..., :bin_count]
    imag_part = as_float[..., bin_count:]
    amplitude = jnp.sqrt(real_part * real_part + imag_part * imag_part + 1e-06)
    positions = jnp.arange(bin_count, dtype=jnp.int32)
    inside = (jnp.abs(positions[:, None] - positions[None, :]) <= SMOOTH).astype(jnp.float32)
    smoothing = inside / jnp.sum(inside, axis=0, keepdims=True)
    smoothed = jnp.matmul(amplitude, smoothing, precision=lax.Precision.HIGHEST)
    return jnp.concatenate([real_part / smoothed, imag_part / smoothed], -1).astype(jnp.bfloat16)


def lag_weights(bin_count, lag_count):
    frequency = jnp.arange(bin_count, dtype=jnp.int32) + FIRST_BIN
    lag_index = jnp.arange(lag_count, dtype=jnp.int32) - lag_count // 2
    phase_index = frequency[:, None] * lag_index[None, :] % SAMPLES
    theta = phase_index.astype(jnp.float32) * (2.0 * math.pi / SAMPLES)
    return jnp.concatenate([jnp.cos(theta), -jnp.sin(theta)], 0).astype(jnp.bfloat16)


def distance_factor(distance_mask, row_first, row_total, block_gap, col_total):
    row_ids = row_first + jnp.arange(row_total, dtype=jnp.int32)
    col_ids = jnp.arange(col_total, dtype=jnp.int32)
    distance = jnp.abs(col_total * block_gap + col_ids[None, :] - row_ids[:, None]).reshape(-1)
    matches = (
        distance[:, None] == jnp.arange(distance_mask.shape[0], dtype=jnp.int32)[None, :]
    ).astype(jnp.float32)
    return jnp.dot(matches, distance_mask.astype(jnp.float32), precision=lax.Precision.HIGHEST)


def cross_kernel(bin_starts, offsets_ref, *refs):
    pieces = refs[:BAND_BLOCKS]
    out_ref, row_buf, col_buf, sems = refs[BAND_BLOCKS:]
    bins = row_buf.shape[1]
    for slot_index in range(SLOTS):
        for side, buf in ((0, row_buf), (1, col_buf)):
            index = offsets_ref[slot_index, side]
            for d in range(BAND_BLOCKS):

                @pl.when(index == d)
                def _start(d=d, buf=buf, side=side):
                    source = pieces[d].at[pl.ds(bin_starts[d], bins)]
                    pltpu.make_async_copy(
                        source, buf.at[slot_index], sems.at[slot_index, side]
                    ).start()

    nt = (((1,), (1,)), ((), ()))

    def dot(a, b):
        return lax.dot_general(a, b, nt, preferred_element_type=jnp.float32)

    for slot_index in range(SLOTS):
        for side, buf in ((0, row_buf), (1, col_buf)):
            source = pieces[0].at[pl.ds(bin_starts[0], bins)]
            pltpu.make_async_copy(source, buf.at[slot_index], sems.at[slot_index, side]).wait()

        def per_bin(f, carry, slot_index=slot_index):
            row_re = row_buf[slot_index, f, 0]
            row_im = row_buf[slot_index, f, 1]
            col_re = col_buf[slot_index, f, 0]
            col_im = col_buf[slot_index, f, 1]
            real_part = dot(row_re, col_re) + dot(row_im, col_im)
            imag_part = dot(row_re, col_im) - dot(row_im, col_re)
            out_ref[slot_index, f, 0] = real_part.astype(out_ref.dtype)
            out_ref[slot_index, f, 1] = imag_part.astype(out_ref.dtype)
            return carry

        lax.fori_loop(0, bins, per_bin, 0)


def cross_slots(offsets, pieces, bin_starts, bins):
    _, _, channels, seg_total = pieces[0].shape
    buffer = pltpu.VMEM((SLOTS, bins, 2, channels, seg_total), jnp.bfloat16)
    return pl.pallas_call(
        functools.partial(cross_kernel, tuple(bin_starts)),
        out_shape=jax.ShapeDtypeStruct((SLOTS, bins, 2, channels, channels), jnp.bfloat16),
        in_specs=[pl.BlockSpec(memory_space=pltpu.SMEM)]
        + [pl.BlockSpec(memory_space=pl.ANY)] * BAND_BLOCKS,
        out_specs=pl.BlockSpec(memory_space=pltpu.VMEM),
        scratch_shapes=[buffer, buffer, pltpu.SemaphoreType.DMA((SLOTS, 2))],
    )(offsets, *pieces)


def site_stack(pieces, bin_starts, bins, pair_lists, site_offset):
    peers = lax.axis_size("pair")
    owner_lists = rotated(pair_lists, "pair", site_offset)[0]
    owner = (lax.axis_index("pair") - site_offset) % peers
    offsets = jnp.clip(owner_lists - owner, 0, BAND_BLOCKS - 1).astype(jnp.int32)
    stacked = cross_slots(offsets, pieces, bin_starts, bins)
    return rotated(stacked, "pair", -site_offset)


def body(spectra, pair_lists, distance_mask):
    group_total = lax.axis_size("seg")
    seg_index = lax.axis_index("seg")
    seg_local, block_width, row_width = spectra.shape
    bin_count = row_width // 2
    group_bins = bin_count // group_total
    row_share = block_width // group_total

    whitened = whiten(spectra)
    by_bins = whitened.reshape(seg_local, block_width, 2, group_total, group_bins)
    by_bins = by_bins.transpose(3, 4, 2, 1, 0)
    far_local = lax.all_to_all(by_bins[:, NEAR_BINS:], "seg", 0, 4, tiled=True)[0]
    near_local = lax.all_to_all(by_bins[:, :NEAR_BINS], "seg", 0, 4, tiled=True)[0]

    far_below = rotated(far_local, "pair", 1)
    far_above = rotated(far_local, "pair", -1)
    far_two_below = rotated(far_below, "pair", 1)
    near_below = rotated(near_local, "pair", 1)
    near_above = rotated(near_local, "pair", -1)
    near_two_above = rotated(near_above, "pair", -1)
    far_bins = group_bins - NEAR_BINS
    far = site_stack(
        (far_two_below, far_below, far_local, far_above), (0, 0, 0, 0), far_bins, pair_lists, 2
    )
    near = site_stack(
        (near_below, near_local, near_above, near_two_above), (0, 0, 0, 0), NEAR_BINS, pair_lists, 1
    )
    stacked_bins = jnp.concatenate([near, far], 1)
    stacked_bins = stacked_bins.reshape(
        SLOTS, group_bins, 2, group_total, row_share, block_width
    )
    stacked_bins = lax.all_to_all(stacked_bins, "seg", 3, 3, tiled=True)
    stacked_all = stacked_bins.transpose(0, 4, 5, 2, 3, 1).reshape(
        SLOTS, row_share, block_width, row_width
    )

    lag_table = lag_weights(bin_count, LAGS)
    scale_norm = 1.0 / math.sqrt(seg_local * group_total * bin_count)
    outputs = []
    for slot_index in range(SLOTS):
        row_block = pair_lists[0, slot_index, 0]
        col_block = pair_lists[0, slot_index, 1]
        is_live = (row_block >= 0).astype(jnp.float32)
        lagged = jnp.dot(
            stacked_all[slot_index].reshape(-1, row_width),
            lag_table,
            preferred_element_type=jnp.float32,
        )
        factor = (
            distance_factor(
                distance_mask, seg_index * row_share, row_share, col_block - row_block, block_width
            )
            * scale_norm
            * is_live
        )
        outputs.append(
            (lagged * factor[:, None]).astype(jnp.bfloat16).reshape(row_share, block_width, LAGS)
        )
    return jnp.stack(outputs, 0)[None]


def solution(mesh):
    in_specs = (P("seg", "pair", None), P("pair", None, None), P())
    out_specs = P("pair", None, "seg", None, None)
    return jax.shard_map(body, mesh=mesh, in_specs=in_specs, out_specs=out_specs, check_vma=False)
```

```python
import functools
import math

import jax
import jax.numpy as jnp
from jax import lax
from jax.experimental import pallas as pl
from jax.experimental.pallas import tpu as pltpu
from jax.sharding import PartitionSpec as P

LAGS = 1025
SAMPLES = 6000
FIRST_BIN = 30
SMOOTH = 4
BAND_BLOCKS = 4
SLOTS = 2
NEAR_BINS = 4


def rotated(array, axis, by):
    peers = lax.axis_size(axis)
    pairs = [(i, (i + by) % peers) for i in range(peers)]
    return lax.ppermute(array, axis, pairs)


def whiten(spectra):
    bin_count = spectra.shape[-1] // 2
    as_float = spectra.astype(jnp.float32)
    real_part = as_float[..., :bin_count]
    imag_part = as_float[..., bin_count:]
    amplitude = jnp.sqrt(real_part * real_part + imag_part * imag_part + 1e-06)
    positions = jnp.arange(bin_count, dtype=jnp.int32)
    inside = (jnp.abs(positions[:, None] - positions[None, :]) <= SMOOTH).astype(jnp.float32)
    smoothing = inside / jnp.sum(inside, axis=0, keepdims=True)
    smoothed = jnp.matmul(amplitude, smoothing, precision=lax.Precision.HIGHEST)
    return jnp.concatenate([real_part / smoothed, imag_part / smoothed], -1).astype(jnp.bfloat16)


def lag_weights(bin_count, lag_count):
    frequency = jnp.arange(bin_count, dtype=jnp.int32) + FIRST_BIN
    lag_index = jnp.arange(lag_count, dtype=jnp.int32) - lag_count // 2
    phase_index = frequency[:, None] * lag_index[None, :] % SAMPLES
    theta = phase_index.astype(jnp.float32) * (2.0 * math.pi / SAMPLES)
    return jnp.concatenate([jnp.cos(theta), -jnp.sin(theta)], 0).astype(jnp.bfloat16)


def distance_factor(distance_mask, row_first, row_total, block_gap, col_total):
    row_ids = row_first + jnp.arange(row_total, dtype=jnp.int32)
    col_ids = jnp.arange(col_total, dtype=jnp.int32)
    distance = jnp.abs(col_total * block_gap + col_ids[None, :] - row_ids[:, None]).reshape(-1)
    matches = (
        distance[:, None] == jnp.arange(distance_mask.shape[0], dtype=jnp.int32)[None, :]
    ).astype(jnp.float32)
    return jnp.dot(matches, distance_mask.astype(jnp.float32), precision=lax.Precision.HIGHEST)


def cross_kernel(bin_starts, offsets_ref, *refs):
    pieces = refs[:BAND_BLOCKS]
    out_ref, row_buf, col_buf, sems = refs[BAND_BLOCKS:]
    bins = row_buf.shape[1]
    for slot_index in range(SLOTS):
        for side, buf in ((0, row_buf), (1, col_buf)):
            index = offsets_ref[slot_index, side]
            for d in range(BAND_BLOCKS):

                @pl.when(index == d)
                def _start(d=d, buf=buf, side=side):
                    source = pieces[d].at[pl.ds(bin_starts[d], bins)]
                    pltpu.make_async_copy(
                        source, buf.at[slot_index], sems.at[slot_index, side]
                    ).start()

    nt = (((1,), (1,)), ((), ()))

    def dot(a, b):
        return lax.dot_general(a, b, nt, preferred_element_type=jnp.float32)

    for slot_index in range(SLOTS):
        for side, buf in ((0, row_buf), (1, col_buf)):
            source = pieces[0].at[pl.ds(bin_starts[0], bins)]
            pltpu.make_async_copy(source, buf.at[slot_index], sems.at[slot_index, side]).wait()

        def per_bin(f, carry, slot_index=slot_index):
            row_re = row_buf[slot_index, f, 0]
            row_im = row_buf[slot_index, f, 1]
            col_re = col_buf[slot_index, f, 0]
            col_im = col_buf[slot_index, f, 1]
            real_part = dot(row_re, col_re) + dot(row_im, col_im)
            imag_part = dot(row_re, col_im) - dot(row_im, col_re)
            out_ref[slot_index, f, 0] = real_part.astype(out_ref.dtype)
            out_ref[slot_index, f, 1] = imag_part.astype(out_ref.dtype)
            return carry

        lax.fori_loop(0, bins, per_bin, 0)


def cross_slots(offsets, pieces, bin_starts, bins):
    _, _, channels, seg_total = pieces[0].shape
    buffer = pltpu.VMEM((SLOTS, bins, 2, channels, seg_total), jnp.bfloat16)
    return pl.pallas_call(
        functools.partial(cross_kernel, tuple(bin_starts)),
        out_shape=jax.ShapeDtypeStruct((SLOTS, bins, 2, channels, channels), jnp.bfloat16),
        in_specs=[pl.BlockSpec(memory_space=pltpu.SMEM)]
        + [pl.BlockSpec(memory_space=pl.ANY)] * BAND_BLOCKS,
        out_specs=pl.BlockSpec(memory_space=pltpu.VMEM),
        scratch_shapes=[buffer, buffer, pltpu.SemaphoreType.DMA((SLOTS, 2))],
    )(offsets, *pieces)


def site_stack(pieces, bin_starts, bins, pair_lists, site_offset):
    peers = lax.axis_size("pair")
    owner_lists = rotated(pair_lists, "pair", site_offset)[0]
    owner = (lax.axis_index("pair") - site_offset) % peers
    offsets = jnp.clip(owner_lists - owner, 0, BAND_BLOCKS - 1).astype(jnp.int32)
    stacked = cross_slots(offsets, pieces, bin_starts, bins)
    return rotated(stacked, "pair", -site_offset)


def body(spectra, pair_lists, distance_mask):
    group_total = lax.axis_size("seg")
    seg_index = lax.axis_index("seg")
    seg_local, block_width, row_width = spectra.shape
    bin_count = row_width // 2
    group_bins = bin_count // group_total
    row_share = block_width // group_total

    whitened = whiten(spectra)
    by_bins = whitened.reshape(seg_local, block_width, 2, group_total, group_bins)
    by_bins = by_bins.transpose(3, 4, 2, 1, 0)
    far_local = lax.all_to_all(by_bins[:, NEAR_BINS:], "seg", 0, 4, tiled=True)[0]
    near_local = lax.all_to_all(by_bins[:, :NEAR_BINS], "seg", 0, 4, tiled=True)[0]

    far_below = rotated(far_local, "pair", 1)
    far_above = rotated(far_local, "pair", -1)
    far_two_below = rotated(far_below, "pair", 1)
    near_below = rotated(near_local, "pair", 1)
    near_above = rotated(near_local, "pair", -1)
    near_two_above = rotated(near_above, "pair", -1)
    far_bins = group_bins - NEAR_BINS
    far = site_stack(
        (far_two_below, far_below, far_local, far_above), (0, 0, 0, 0), far_bins, pair_lists, 2
    )
    near = site_stack(
        (near_below, near_local, near_above, near_two_above), (0, 0, 0, 0), NEAR_BINS, pair_lists, 1
    )
    by_rows = []
    for site_part in (near, far):
        site_part = site_part.reshape(
            SLOTS, site_part.shape[1], 2, group_total, row_share, block_width
        )
        by_rows.append(lax.all_to_all(site_part, "seg", 3, 3, tiled=True))
    stacked_bins = jnp.concatenate(by_rows, 1)
    stacked_all = stacked_bins.transpose(0, 4, 5, 2, 3, 1).reshape(
        SLOTS, row_share, block_width, row_width
    )

    lag_table = lag_weights(bin_count, LAGS)
    scale_norm = 1.0 / math.sqrt(seg_local * group_total * bin_count)
    outputs = []
    for slot_index in range(SLOTS):
        row_block = pair_lists[0, slot_index, 0]
        col_block = pair_lists[0, slot_index, 1]
        is_live = (row_block >= 0).astype(jnp.float32)
        lagged = jnp.dot(
            stacked_all[slot_index].reshape(-1, row_width),
            lag_table,
            preferred_element_type=jnp.float32,
        )
        factor = (
            distance_factor(
                distance_mask, seg_index * row_share, row_share, col_block - row_block, block_width
            )
            * scale_norm
            * is_live
        )
        outputs.append(
            (lagged * factor[:, None]).astype(jnp.bfloat16).reshape(row_share, block_width, LAGS)
        )
    return jnp.stack(outputs, 0)[None]


def solution(mesh):
    in_specs = (P("seg", "pair", None), P("pair", None, None), P())
    out_specs = P("pair", None, "seg", None, None)
    return jax.shard_map(body, mesh=mesh, in_specs=in_specs, out_specs=out_specs, check_vma=False)
```
